32 devices in a mesh: rows: 8 (over z, x), cores: 4 (over y, core).
Axes of the slice: x: 2, y: 2, z: 4, core: 2. Of those that a mesh axis runs over, the one named last changes fastest.
Arguments:
- factor_one: bfloat16 [65536, 256], P(('rows', 'cores')), may hold values from -0.375 to 0.375
- factor_two: bfloat16 [65536, 256], P(('rows', 'cores')), may hold values from -0.375 to 0.375
- middle_one: float32 [256, 256], replicated, may hold values from -0.375 to 0.375
- middle_two: float32 [256, 256], replicated, may hold values from -0.375 to 0.375
- directions: float32 [8, 65536], P(None, ('rows', 'cores')), may hold values from -6 to 6
- residual: float32 [8, 65536], P(None, ('rows', 'cores')), may hold values from -6 to 6
Outputs:
- products: float32 [8, 65536], P(None, ('rows', 'cores'))
- gradient: float32 [65536, 256], P(('rows', 'cores'))
The draws below stay inside these ranges and needn't reach their ends.
All inputs are finite; a program needn't handle non-finite values.
Results may differ from the reference program's by a relative error of at most 0.0041.
Values sent between devices are 32-bit elements; how exact they have to be, the bound alone decides.
No kernel may reach another device: no remote copies, remote signals or barrier semaphores. Data moves between devices by JAX's collectives and lax.ppermute only.
A program may use at most 64 MiB of HBM per device.

```python
import jax
import jax.numpy as jnp
from jax import lax

RANK = 256
PROBES = 8
ROWS = 65536


def shard_levels(rng, extent, shards, low, top_value):
    gain = 1.0
    for dim, blocks in shards:
        steps = jax.random.uniform(jax.random.fold_in(jax.random.fold_in(rng, 6), dim), (blocks,), jnp.float32, low / len(shards), top_value / len(shards))
        gain = gain * jnp.repeat(jnp.exp(steps), extent[dim] // blocks).reshape((-1,) + (1,) * (len(extent) - 1 - dim))
    return gain


def gaussian(own_key, extent, deviation, limit, cuts=(), held_as=jnp.bfloat16):
    drawn = jax.random.normal(own_key, extent, jnp.float32) * deviation
    if len(cuts) > 0:
        drawn = shard_levels(own_key, extent, cuts, -0.22, 0.18) * drawn
    return jnp.clip(drawn, min=-limit, max=limit).astype(held_as)


def setup_inputs(seed: int = 0) -> dict:
    splits = jax.random.split(jax.random.key(seed), 7)
    return {
        "factor_one": gaussian(splits[0], (ROWS, RANK), RANK ** -0.5, 0.375, ((0, 32),)),
        "factor_two": gaussian(splits[1], (ROWS, RANK), RANK ** -0.5, 0.375, ((0, 32),)),
        "middle_one": gaussian(splits[2], (RANK, RANK), RANK ** -0.5, 0.375, (), jnp.float32),
        "middle_two": gaussian(splits[3], (RANK, RANK), RANK ** -0.5, 0.375, (), jnp.float32),
        "directions": gaussian(splits[4], (PROBES, ROWS), 1.0, 6.0, ((1, 32),), jnp.float32),
        "residual": gaussian(splits[5], (PROBES, ROWS), 1.0, 6.0, ((1, 32),), jnp.float32),
    }


def build_cores(factor_one, factor_two, weights):
    upper = factor_one.astype(jnp.float32)
    lower = factor_two.astype(jnp.float32)

    def single(row_weights):
        scaled = (row_weights[:, None] * lower).astype(jnp.bfloat16)
        scaled = lax.optimization_barrier(scaled).astype(jnp.float32)
        return jnp.einsum("nb,nd->bd", upper, scaled, precision=lax.Precision.HIGHEST)

    return lax.map(single, weights)


def transform(cores, left_side, right_side):
    halfway = jnp.einsum("pbd,ed->pbe", cores, right_side, precision=lax.Precision.HIGHEST)
    return jnp.einsum("ab,pbe->pae", left_side, halfway, precision=lax.Precision.HIGHEST)


def reference(factor_one, factor_two, middle_one, middle_two, directions, residual):
    upper = factor_one.astype(jnp.float32)
    lower = factor_two.astype(jnp.float32)
    g_core = transform(build_cores(factor_one, factor_two, directions), middle_one, middle_two).astype(jnp.bfloat16)

    def apply_one(g_single):
        return jnp.sum(jnp.dot(upper, g_single.astype(jnp.float32), precision=lax.Precision.HIGHEST) * lower, axis=1)

    products = lax.map(apply_one, g_core)
    h_core = transform(build_cores(factor_one, factor_two, residual), middle_one.T, middle_two.T).astype(jnp.bfloat16)
    gradient = jnp.zeros(upper.shape, jnp.float32)
    for probe in range(PROBES):
        g_rows = jnp.dot(lower, g_core[probe].astype(jnp.float32).T, precision=lax.Precision.HIGHEST)
        h_rows = jnp.dot(lower, h_core[probe].astype(jnp.float32).T, precision=lax.Precision.HIGHEST)
        gradient = gradient + residual[probe][:, None] * g_rows + directions[probe][:, None] * h_rows
    return products, gradient
```

```python
import functools
import jax
import jax.numpy as jnp
from jax import lax
from jax.experimental import pallas as pl
from jax.experimental.pallas import tpu as pltpu
from jax.sharding import PartitionSpec as P

AXES = ("rows", "cores")
VMEM = pl.BlockSpec(memory_space=pltpu.VMEM)
SMEM = pl.BlockSpec(memory_space=pltpu.SMEM)
TILE = 256

GROUPS = ((3, (2, 1, 3, 4), "h"), (3, (1, 3, 2, 4), "h"), (2, (3, 2, 4, 1), "d"))

NT = (((1,), (1,)), ((), ()))


def bit_of(me, bit):
    return lax.rem(lax.shift_right_logical(me, bit), 2)


def dot3(a, b):
    a_hi = a.astype(jnp.bfloat16)
    a_lo = (a - a_hi.astype(jnp.float32)).astype(jnp.bfloat16)
    b_hi = b.astype(jnp.bfloat16)
    b_lo = (b - b_hi.astype(jnp.float32)).astype(jnp.bfloat16)
    dot = functools.partial(lax.dot_general, dimension_numbers=NT, preferred_element_type=jnp.float32)
    return dot(a_hi, b_hi) + (dot(a_hi, b_lo) + dot(a_lo, b_hi))


def pieces(count, bits, mode, block):
    quarter = block // 4
    for r1 in range(2):
        for r2 in range(2):
            if mode == "h":
                for r3 in range(2):
                    for m in range(count):
                        yield r1 * 2 + r2, r3 * count * (quarter // 2) + m * (quarter // 2), quarter // 2, m, (r1, r2, r3)
            else:
                for m in range(count):
                    yield r1 * 2 + r2, m * quarter, quarter, m, (r1, r2)


def offset(me, bits, rel, block):
    total = 0
    size = block
    for bit, r in zip(bits, rel):
        size //= 2
        mine = bit_of(me, bit)
        total = total + (mine if r == 0 else 1 - mine) * size
    return total


def core_kernel(items, mine, half, s_ref, f1_ref, f2_ref, dirs_ref, res_ref, out_ref):
    core = bit_of(s_ref[0], 0)
    base = (core if mine else 1 - core) * half
    rank = f2_ref.shape[1]
    for k in range(f1_ref.shape[0] // TILE):
        rows = pl.ds(k * TILE, TILE)
        f2t = f2_ref[rows, :].astype(jnp.float32).T
        parts = []
        for kind, probe in items:
            w = (dirs_ref if kind == 0 else res_ref)[pl.ds(base + probe, 1), rows]
            parts.append((f2t * w).astype(jnp.bfloat16))
        r = jnp.dot(jnp.concatenate(parts, axis=0), f1_ref[rows, :], preferred_element_type=jnp.float32)
        if k == 0:
            out_ref[...] = r
        else:
            out_ref[...] += r


def build(items, mine, half, me, f1, f2, dirs, res):
    rank = f1.shape[1]
    m = len(items)
    return pl.pallas_call(
        functools.partial(core_kernel, items, mine, half),
        out_shape=jax.ShapeDtypeStruct((m * f2.shape[1], rank), jnp.float32),
        in_specs=[SMEM] + [VMEM] * 4,
        out_specs=VMEM,
        name=f"cores_{'own' if mine else 'other'}",
        cost_estimate=pl.CostEstimate(
            flops=2 * m * f1.shape[0] * rank * rank, bytes_accessed=f1.size * 4 + m * rank * rank * 4, transcendentals=0
        ),
    )(me, f1, f2, dirs, res)


def transform_kernel(items, bits, mode, s_ref, a_ref, b_ref, m1_ref, m2_ref, m1t_ref, m2t_ref, q0, q1, q2, q3, scr):
    me = s_ref[0]
    qs = (q0, q1, q2, q3)
    rank = m1_ref.shape[0]
    m = len(items)
    for j, (kind, _) in enumerate(items):
        ct = a_ref[j * rank:(j + 1) * rank, :] + b_ref[j * rank:(j + 1) * rank, :]
        left, right = (m1_ref, m2_ref) if kind == 0 else (m1t_ref, m2t_ref)
        scr[j * rank:(j + 1) * rank, :] = dot3(dot3(left[...], ct), right[...])
    for q, row, size, j, rel in pieces(m, bits, mode, rank):
        off = pl.multiple_of(offset(me, bits, rel, rank), 32)
        qs[q][row:row + size, :] = scr[pl.ds(j * rank + off, size), :]


def transform(items, bits, mode, me, own, got, m1, m2, m1t, m2t):
    rank = m1.shape[0]
    m = len(items)
    return pl.pallas_call(
        functools.partial(transform_kernel, items, bits, mode),
        out_shape=[jax.ShapeDtypeStruct((m * rank // 4, rank), jnp.float32)] * 4,
        in_specs=[SMEM] + [VMEM] * 6,
        out_specs=[VMEM] * 4,
        scratch_shapes=[pltpu.VMEM((m * rank, rank), jnp.float32)],
        name="transform",
        cost_estimate=pl.CostEstimate(flops=12 * m * rank**3, bytes_accessed=12 * m * rank * rank, transcendentals=0),
    )(me, own, got, m1, m2, m1t, m2t)


def apply_kernel(parts, half, first, last, n_in, *refs):
    s_ref, f1_ref, f2_ref, dirs_ref, res_ref = refs[:5]
    pos = 5
    fs = []
    for _ in parts:
        fs.append(refs[pos:pos + 4])
        pos += 4
    if not first:
        acc_in, prod_in = refs[pos:pos + 2]
        pos += 2
    acc_ref, prod_ref = refs[pos:pos + 2]
    pos += 2
    if last:
        acc_ref, grad_ref = acc_in, acc_ref
    g_ref = refs[pos]
    me = s_ref[0]
    core = bit_of(me, 0)
    rank = f2_ref.shape[1]
    todo = []
    start = 0
    for (items, bits, mode, mine), f in zip(parts, fs):
        for q, row, size, j, rel in pieces(len(items), bits, mode, rank):
            off = pl.multiple_of(offset(me, bits, rel, rank), 32)
            g_ref[pl.ds(start + j * rank + off, size), :] = f[q][row:row + size, :].astype(jnp.bfloat16)
        base = (core if mine else 1 - core) * half
        for kind, probe in items:
            todo.append((kind, base + probe, start))
            start += rank
    if not first:
        prod_ref[...] = prod_in[...]

    def tile(k, carry):
        rows = pl.ds(pl.multiple_of(k * TILE, TILE), TILE)
        f2 = f2_ref[rows, :]
        f1t = f1_ref[rows, :].astype(jnp.float32).T
        total = None if first else acc_in[:, rows]
        for kind, probe, at in todo:
            r = lax.dot_general(g_ref[at:at + rank, :], f2, NT, preferred_element_type=jnp.float32)
            w = (res_ref if kind == 0 else dirs_ref)[pl.ds(probe, 1), rows]
            term = r * w
            total = term if total is None else total + term
            if kind == 0:
                prod_ref[pl.ds(probe, 1), rows] = jnp.sum(r * f1t, axis=0, keepdims=True)
        if last:
            grad_ref[rows, :] = total.T
        else:
            acc_ref[:, rows] = total
        return carry

    lax.fori_loop(0, f2_ref.shape[0] // TILE, tile, 0)


def apply_cores(parts, half, me, f1, f2, dirs, res, blocks, state, last):
    n, rank = f1.shape
    first = state is None
    total = sum(len(p[0]) for p in parts)
    ops = [me, f1, f2, dirs, res] + [b for four in blocks for b in four] + ([] if first else list(state))
    acc = jax.ShapeDtypeStruct((n, rank) if last else (rank, n), jnp.float32)
    aliases = {}
    if not first:
        aliases = {len(ops) - 1: 1}
        if not last:
            aliases[len(ops) - 2] = 0
    return pl.pallas_call(
        functools.partial(apply_kernel, parts, half, first, last, len(ops)),
        out_shape=[acc, jax.ShapeDtypeStruct(dirs.shape, jnp.float32)],
        in_specs=[SMEM] + [VMEM] * (len(ops) - 1),
        out_specs=[VMEM] * 2,
        scratch_shapes=[pltpu.VMEM((total * rank, rank), jnp.bfloat16)],
        input_output_aliases=aliases,
        name="apply_last" if last else "apply",
        cost_estimate=pl.CostEstimate(flops=2 * total * n * rank * rank, bytes_accessed=8 * n * rank, transcendentals=0),
    )(*ops)


def shards(count, factor_one, factor_two, middle_one, middle_two, directions, residual):
    half = directions.shape[0] // 2
    extra = tuple(range(5, count.bit_length() - 1))

    def swap(x, bit):
        return lax.ppermute(x, AXES, [(i, i ^ (1 << bit)) for i in range(count)])

    me = (lax.axis_index("rows") * lax.axis_size("cores") + lax.axis_index("cores")).astype(jnp.int32).reshape(1)
    m1t, m2t = middle_one.T, middle_two.T
    items = [(j % 2, j // 2) for j in range(2 * half)]
    groups = []
    at = 0
    for i, (size, bits, mode) in enumerate(GROUPS):
        size = len(items) - at if i == len(GROUPS) - 1 else size
        groups.append((tuple(items[at:at + size]), bits, mode))
        at += size
    args = (me, factor_one, factor_two, directions, residual)

    q = []
    for its, bits, mode in groups:
        other = build(its, False, half, *args)
        got = swap(other, 0)
        own = build(its, True, half, *args)
        q.append(transform(its, bits, mode, me, own, got, middle_one, middle_two, m1t, m2t))
    t = [{} for _ in groups]
    for (_, bits, mode), v, x in zip(groups, t, q):
        v["r11"] = swap(x[3], bits[0])
    for (_, bits, mode), v, x in zip(groups, t, q):
        v["r10"] = swap(x[2], bits[0])
    for (_, bits, mode), v, x in zip(groups, t, q):
        v["r01"] = swap(x[1] + v["r11"], bits[1])
    for (_, bits, mode), v, x in zip(groups, t, q):
        a, b, c = x[0], v["r10"], v["r01"]
        if mode == "h":
            h = a.shape[0] // 2
            v["k"] = (a[:h] + b[:h]) + c[:h]
            v["r3"] = swap((a[h:] + b[h:]) + c[h:], bits[2])
        else:
            v["k"] = (a + b) + c
            v["r3"] = swap(v["k"], bits[2])
    for (_, bits, mode), v in zip(groups, t):
        v["k"] = v["k"] + v["r3"]
        v["r4"] = swap(v["k"], bits[3])
    for bit in extra:
        for v in t:
            v["k"] = v["k"] + v["r4"]
            v["r4"] = swap(v["k"], bit)
    for (_, bits, mode), v in zip(groups, t):
        v["k"] = v["k"] + v["r4"]
        if mode == "h":
            v["k"] = jnp.concatenate([v["k"], swap(v["k"], bits[2])])
    for (_, bits, mode), v in zip(groups, t):
        v["f01"] = swap(v["k"], bits[1])
        v["f10"] = swap(v["k"], bits[0])
    for (_, bits, mode), v in zip(groups, t):
        v["f11"] = swap(v["f01"], bits[0])
        v["f"] = [v["k"], v["f01"], v["f10"], v["f11"]]
        v["o"] = [swap(x, 0) for x in v["f"]]
    state = None
    for i, ((its, bits, mode), v) in enumerate(zip(groups, t)):
        parts = [(its, bits, mode, True), (its, bits, mode, False)]
        state = apply_cores(
            parts, half, me, factor_one, factor_two, directions, residual, [v["f"], v["o"]], state, i == len(groups) - 1
        )
    gradient, products = state
    return products, gradient


def solution(mesh):
    placed = (
        P(AXES, None),
        P(AXES, None),
        P(),
        P(),
        P(None, AXES),
        P(None, AXES),
    )
    count = mesh.shape["rows"] * mesh.shape["cores"]
    return jax.shard_map(
        functools.partial(shards, count),
        mesh=mesh,
        in_specs=placed,
        out_specs=(P(None, AXES), P(AXES, None)),
        check_vma=False,
    )
```

```python
import functools
import jax
import jax.numpy as jnp
from jax import lax
from jax.experimental import pallas as pl
from jax.experimental.pallas import tpu as pltpu
from jax.sharding import PartitionSpec as P


AXES = ("rows", "cores")
VMEM = pl.BlockSpec(memory_space=pltpu.VMEM)
SMEM = pl.BlockSpec(memory_space=pltpu.SMEM)
TILE = 256
LOADS = 4
STAGES = ((0,), (1, 2), (3,))

GROUPS = ((3, (2, 1, 3, 4), "h"), (3, (1, 3, 2, 4), "h"), (2, (3, 2, 4, 1), "d"))

NT = (((1,), (1,)), ((), ()))


def bit_of(me, bit):
    return lax.rem(lax.shift_right_logical(me, bit), 2)


def split(x):
    high = x.astype(jnp.bfloat16)
    return high, (x - high.astype(jnp.float32)).astype(jnp.bfloat16)


def dot3(a, b):
    dot = functools.partial(lax.dot_general, dimension_numbers=NT, preferred_element_type=jnp.float32)
    return dot(a[0], b[0]) + (dot(a[0], b[1]) + dot(a[1], b[0]))


def blocks(count, mode, rank):
    quarter = rank // 4
    if mode == "d":
        return [(m * quarter, quarter, (), m) for m in range(count)]
    half = quarter // 2
    return [((r3 * count + m) * half, half, (r3,), m) for r3 in range(2) for m in range(count)]


def offset(me, bits, rel, block):
    total = 0
    size = block
    for bit, r in zip(bits, rel):
        size //= 2
        mine = bit_of(me, bit)
        total = total + (mine if r == 0 else 1 - mine) * size
    return total


def weighted(items, base, dirs_ref, res_ref, f2t, rows):
    parts = []
    for kind, probe in items:
        w = (dirs_ref if kind == 0 else res_ref)[pl.ds(base + probe, 1), rows]
        parts.append((f2t * w).astype(jnp.bfloat16))
    return jnp.concatenate(parts, axis=0)


def open_kernel(items, half, s_ref, f1_in, f2_in, dirs_in, res_in, out_ref, f1_ref, f2t_ref, dirs_ref, res_ref, f2_ref, sems):
    base = (1 - bit_of(s_ref[0], 0)) * half
    size = f1_in.shape[0] // LOADS
    small = [
        pltpu.make_async_copy(dirs_in, dirs_ref, sems.at[0]),
        pltpu.make_async_copy(res_in, res_ref, sems.at[1]),
    ]
    big = []
    for i in range(LOADS):
        part = pl.ds(i * size, size)
        big.append((
            pltpu.make_async_copy(f2_in.at[part], f2_ref.at[part], sems.at[2 + 2 * i]),
            pltpu.make_async_copy(f1_in.at[part], f1_ref.at[part], sems.at[3 + 2 * i]),
        ))
    for copy in small + [c for two in big for c in two]:
        copy.start()
    for copy in small:
        copy.wait()
    for k in range(f1_in.shape[0] // TILE):
        if k * TILE % size == 0:
            for copy in big[k * TILE // size]:
                copy.wait()
        rows = pl.ds(k * TILE, TILE)
        f2t = f2_ref[rows, :].astype(jnp.float32).T
        f2t_ref[:, rows] = f2t.astype(jnp.bfloat16)
        st = weighted(items, base, dirs_ref, res_ref, f2t, rows)
        r = jnp.dot(st, f1_ref[rows, :], preferred_element_type=jnp.float32)
        if k == 0:
            out_ref[...] = r
        else:
            out_ref[...] += r


def open_build(items, half, me, f1, f2, dirs, res):
    n, rank = f1.shape
    m = len(items)
    hbm = pl.BlockSpec(memory_space=pltpu.HBM)
    return pl.pallas_call(
        functools.partial(open_kernel, items, half),
        out_shape=[
            jax.ShapeDtypeStruct((m * rank, rank), jnp.float32),
            jax.ShapeDtypeStruct((n, rank), jnp.bfloat16),
            jax.ShapeDtypeStruct((rank, n), jnp.bfloat16),
            jax.ShapeDtypeStruct(dirs.shape, jnp.float32),
            jax.ShapeDtypeStruct(res.shape, jnp.float32),
        ],
        in_specs=[SMEM] + [hbm] * 4,
        out_specs=[VMEM] * 5,
        scratch_shapes=[pltpu.VMEM((n, rank), jnp.bfloat16), pltpu.SemaphoreType.DMA((2 + 2 * LOADS,))],
        compiler_params=pltpu.CompilerParams(vmem_limit_bytes=10 << 20),
        name="cores_open",
        cost_estimate=pl.CostEstimate(flops=2 * m * n * rank * rank, bytes_accessed=n * rank * 4, transcendentals=0),
    )(me, *(pltpu.with_memory_space_constraint(x, pltpu.HBM) for x in (f1, f2, dirs, res)))


def core_kernel(items, mine, half, s_ref, f1_ref, f2t_ref, dirs_ref, res_ref, *refs):
    out_ref = refs[-1]
    core = bit_of(s_ref[0], 0)
    base = (core if mine else 1 - core) * half
    for k in range(f1_ref.shape[0] // TILE):
        rows = pl.ds(k * TILE, TILE)
        st = weighted(items, base, dirs_ref, res_ref, f2t_ref[:, rows].astype(jnp.float32), rows)
        r = jnp.dot(st, f1_ref[rows, :], preferred_element_type=jnp.float32)
        if k == 0:
            out_ref[...] = r
        else:
            out_ref[...] += r


def build(items, mine, half, after, me, f1, f2t, dirs, res):
    n, rank = f1.shape
    m = len(items)
    extra = [] if after is None else [after]
    return pl.pallas_call(
        functools.partial(core_kernel, items, mine, half),
        out_shape=jax.ShapeDtypeStruct((m * rank, rank), jnp.float32),
        in_specs=[SMEM] + [VMEM] * 4 + [pl.BlockSpec(memory_space=pl.ANY)] * len(extra),
        out_specs=VMEM,
        compiler_params=pltpu.CompilerParams(vmem_limit_bytes=8 << 20),
        cost_estimate=pl.CostEstimate(flops=2 * m * n * rank * rank, bytes_accessed=n * rank * 4, transcendentals=0),
    )(me, f1, f2t, dirs, res, *extra)


def left_kernel(items, bits, mode, s_ref, a_ref, b_ref, m1_ref, q0, q1, q2, q3, scr):
    me = s_ref[0]
    qs = (q0, q1, q2, q3)
    rank = m1_ref.shape[0]
    m = len(items)
    m1 = m1_ref[...]
    sides = (split(m1), split(m1.T))
    for j, (kind, _) in enumerate(items):
        ct = a_ref[j * rank:(j + 1) * rank, :] + b_ref[j * rank:(j + 1) * rank, :]
        scr[j * rank:(j + 1) * rank, :] = dot3(sides[kind], split(ct))
    for r1 in range(2):
        for r2 in range(2):
            for row, size, r3, j in blocks(m, mode, rank):
                off = pl.multiple_of(offset(me, bits, (r1, r2) + r3, rank), 32)
                qs[r1 * 2 + r2][row:row + size, :] = scr[pl.ds(j * rank + off, size), :]


def left(items, bits, mode, me, own, got, m1):
    rank = m1.shape[0]
    m = len(items)
    return pl.pallas_call(
        functools.partial(left_kernel, items, bits, mode),
        out_shape=[jax.ShapeDtypeStruct((m * rank // 4, rank), jnp.float32)] * 4,
        in_specs=[SMEM] + [VMEM] * 3,
        out_specs=[VMEM] * 4,
        scratch_shapes=[pltpu.VMEM((m * rank, rank), jnp.float32)],
        compiler_params=pltpu.CompilerParams(vmem_limit_bytes=8 << 20),
        name="left",
        cost_estimate=pl.CostEstimate(flops=6 * m * rank**3, bytes_accessed=12 * m * rank * rank, transcendentals=0),
    )(me, own, got, m1)


def right_kernel(items, a_ref, b_ref, m2_ref, out_ref):
    rows = a_ref.shape[0] // len(items)
    m2 = m2_ref[...]
    sides = (split(m2), split(m2.T))
    for j, (kind, _) in enumerate(items):
        at = pl.ds(j * rows, rows)
        out_ref[at, :] = dot3(split(a_ref[at, :] + b_ref[at, :]), sides[kind])


def right(items, a, b, m2):
    return pl.pallas_call(
        functools.partial(right_kernel, items),
        out_shape=jax.ShapeDtypeStruct(a.shape, jnp.float32),
        in_specs=[VMEM] * 3,
        out_specs=VMEM,
        compiler_params=pltpu.CompilerParams(vmem_limit_bytes=4 << 20),
        name="right",
        cost_estimate=pl.CostEstimate(flops=6 * a.size * a.shape[1], bytes_accessed=12 * a.size, transcendentals=0),
    )(a, b, m2)


def apply_kernel(parts, half, first, last, *refs):
    s_ref, f1_ref, f2t_ref, dirs_ref, res_ref = refs[:5]
    pos = 5
    arrays = []
    for p in parts:
        arrays.append(refs[pos:pos + len(p[4])])
        pos += len(p[4])
    if not first:
        acc_in, prod_in = refs[pos:pos + 2]
        pos += 2
    acc_ref, prod_ref = refs[pos:pos + 2]
    pos += 2
    if last:
        acc_ref, grad_ref = acc_in, acc_ref
    if first:
        f1t_ref = refs[pos]
        pos += 1
        acc_ref[...] = jnp.zeros_like(acc_ref)
        prod_ref[...] = jnp.zeros_like(prod_ref)
    else:
        f1t_ref = f1_ref
        prod_ref[...] = prod_in[...]
    g_ref, r_ref = refs[pos:pos + 2]
    me = s_ref[0]
    core = bit_of(me, 0)
    rank = f2t_ref.shape[0]
    at = 0
    spans = []
    for four in arrays:
        for f in four:
            g_ref[at:at + f.shape[0], :] = f[...].astype(jnp.bfloat16)
            spans.append((at, f.shape[0]))
            at += f.shape[0]

    def tile(k):
        rows = pl.ds(k * TILE, TILE)
        r_ref[k % 2] = jnp.dot(g_ref[...], f2t_ref[:, rows], preferred_element_type=jnp.float32)
        if first:
            f1t_ref[:, rows] = f1_ref[rows, :].astype(jnp.float32).T
        span = iter(spans)
        for items, bits, mode, mine, quarters in parts:
            base = (core if mine else 1 - core) * half
            w = [(res_ref if kind == 0 else dirs_ref)[pl.ds(base + probe, 1), rows] for kind, probe in items]
            prods = [None] * len(items)
            for q in quarters:
                start, _ = next(span)
                sums = {}
                for row, size, r3, j in blocks(len(items), mode, rank):
                    block = r_ref[k % 2, start + row:start + row + size, :]
                    off = pl.multiple_of(offset(me, bits, (q // 2, q % 2) + r3, rank), 32)
                    term = block * w[j]
                    sums[r3] = (off, size, term if r3 not in sums else sums[r3][2] + term)
                    if items[j][0] == 0:
                        p = block * f1t_ref[pl.ds(off, size), rows]
                        p = jnp.sum(p.reshape(size // 8, 8, TILE), axis=0)
                        prods[j] = p if prods[j] is None else prods[j] + p
                for off, size, total in sums.values():
                    acc_ref[pl.ds(off, size), rows] += total
            for (kind, probe), p in zip(items, prods):
                if kind == 0:
                    prod_ref[pl.ds(base + probe, 1), rows] += jnp.sum(p, axis=0, keepdims=True)
        if last:
            grad_ref[rows, :] = acc_ref[:, rows].T

    for k in range(f2t_ref.shape[1] // TILE):
        tile(k)


def apply_cores(parts, half, me, f1, f2t, dirs, res, state, last):
    rank, n = f2t.shape
    first = state is None
    arrays = [a for p in parts for a in p[4].values()]
    shapes = [p[:4] + (tuple(p[4]),) for p in parts]
    total = sum(a.shape[0] for a in arrays)
    ops = [me, f1, f2t, dirs, res] + arrays + ([] if first else list(state))
    acc = jax.ShapeDtypeStruct((n, rank) if last else (rank, n), jnp.float32)
    outs = [acc, jax.ShapeDtypeStruct(dirs.shape, jnp.float32)]
    aliases = {}
    if first:
        outs.append(jax.ShapeDtypeStruct((rank, n), jnp.float32))
    else:
        aliases = {len(ops) - 1: 1}
        if not last:
            aliases[len(ops) - 2] = 0
    return pl.pallas_call(
        functools.partial(apply_kernel, shapes, half, first, last),
        out_shape=outs,
        in_specs=[SMEM] + [VMEM] * (len(ops) - 1),
        out_specs=[VMEM] * len(outs),
        scratch_shapes=[pltpu.VMEM((total, rank), jnp.bfloat16), pltpu.VMEM((2, total, TILE), jnp.float32)],
        input_output_aliases=aliases,
        compiler_params=pltpu.CompilerParams(vmem_limit_bytes=16 << 20),
        name="apply_last" if last else "apply",
        cost_estimate=pl.CostEstimate(flops=2 * total * n * rank, bytes_accessed=8 * n * rank, transcendentals=0),
    )(*ops)


def shards(count, factor_one, factor_two, middle_one, middle_two, directions, residual):
    half = directions.shape[0] // 2
    extra = tuple(range(5, count.bit_length() - 1))

    def swap(x, bit):
        return lax.ppermute(x, AXES, [(i, i ^ (1 << bit)) for i in range(count)])

    me = (lax.axis_index("rows") * lax.axis_size("cores") + lax.axis_index("cores")).astype(jnp.int32).reshape(1)
    items = [(j % 2, j // 2) for j in range(2 * half)]
    groups = []
    at = 0
    for i, (size, bits, mode) in enumerate(GROUPS):
        size = len(items) - at if i == len(GROUPS) - 1 else size
        groups.append((tuple(items[at:at + size]), bits, mode))
        at += size

    other, f1, f2t, dirs, res = open_build(groups[0][0], half, me, factor_one, factor_two, directions, residual)
    args = (me, f1, f2t, dirs, res)
    others = [swap(other, 0)]
    q, after = [], None
    for g, (its, bits, mode) in enumerate(groups):
        own = build(its, True, half, after, *args)
        if g + 1 < len(groups):
            other = build(groups[g + 1][0], False, half, own, *args)
            others.append(swap(other, 0))
        q.append(left(its, bits, mode, me, own, others[g], middle_one))
        after = q[-1][3]
    t = [{} for _ in groups]
    for (_, bits, mode), v, x in zip(groups, t, q):
        v["r11"] = swap(x[3], bits[0])
    for (_, bits, mode), v, x in zip(groups, t, q):
        v["r10"] = swap(x[2], bits[0])
    for (_, bits, mode), v, x in zip(groups, t, q):
        v["r01"] = swap(x[1] + v["r11"], bits[1])
    for (_, bits, mode), v, x in zip(groups, t, q):
        a, b, c = x[0], v["r10"], v["r01"]
        if mode == "h":
            h = a.shape[0] // 2
            v["k"] = (a[:h] + b[:h]) + c[:h]
            v["s"] = (a[h:] + b[h:]) + c[h:]
        else:
            v["s"] = v["k"] = (a + b) + c
        v["r3"] = swap(v["s"], bits[2])
    for (_, bits, mode), v in zip(groups, t):
        v["k"] = v["k"] + v["r3"]
        v["r4"] = swap(v["k"], bits[3])
    for bit in extra:
        for v in t:
            v["k"] = v["k"] + v["r4"]
            v["r4"] = swap(v["k"], bit)
    for (its, bits, mode), v in zip(groups, t):
        v["k"] = right(its, v["k"], v["r4"], middle_two)
        if mode == "h":
            v["k"] = jnp.concatenate([v["k"], swap(v["k"], bits[2])])
    for (_, bits, mode), v in zip(groups, t):
        v["f"] = {0: v["k"]}
        v["f"][1] = swap(v["k"], bits[1])
        v["f"][2] = swap(v["k"], bits[0])
    for (_, bits, mode), v in zip(groups, t):
        v["f"][3] = swap(v["f"][1], bits[0])
        v["o"] = {}
        for i in range(4):
            v["o"][i] = swap(v["f"][i], 0)
    state = None
    for i, stage in enumerate(STAGES):
        parts = []
        for mine in (True, False):
            for (its, bits, mode), v in zip(groups, t):
                arrays = v["f" if mine else "o"]
                parts.append((its, bits, mode, mine, {j: arrays[j] for j in stage}))
        state = apply_cores(
            parts, half, me, f1, f2t, dirs, res, state, i == len(STAGES) - 1
        )
        if i == 0:
            f1, state = state[2], state[:2]
    gradient, products = state
    return products, gradient


def whole(count, *args):
    return shards(count, *args)


def solution(mesh):
    placed = (
        P(AXES, None),
        P(AXES, None),
        P(),
        P(),
        P(None, AXES),
        P(None, AXES),
    )
    count = mesh.shape["rows"] * mesh.shape["cores"]
    return jax.shard_map(
        functools.partial(whole, count),
        mesh=mesh,
        in_specs=placed,
        out_specs=(P(None, AXES), P(AXES, None)),
        check_vma=False,
    )
```

```python
import functools
import jax
import jax.numpy as jnp
from jax import lax
from jax.experimental import pallas as pl
from jax.experimental.pallas import tpu as pltpu
from jax.sharding import PartitionSpec as P


AXES = ("rows", "cores")
VMEM = pl.BlockSpec(memory_space=pltpu.VMEM)
SMEM = pl.BlockSpec(memory_space=pltpu.SMEM)
TILE = 256
LOADS = 4

GROUPS = ((3, (2, 1, 3, 4), 'h', 'p'), (3, (1, 3, 2, 4), 'h', 'p'), (2, (3, 2, 1, 4), 'h', 'p'))
N = len(GROUPS)
BOTH = (True, False)
STAGES = (
    tuple((g, j, m) for g in range(N) for j in (0, 1, 2) for m in BOTH),
    tuple((g, 3, True) for g in range(N)),
    tuple((g, 3, False) for g in range(N)),
)

NT = (((1,), (1,)), ((), ()))


def bit_of(me, bit):
    return lax.rem(lax.shift_right_logical(me, bit), 2)


def split(x):
    high = x.astype(jnp.bfloat16)
    return high, (x - high.astype(jnp.float32)).astype(jnp.bfloat16)


def dot3(a, b):
    dot = functools.partial(lax.dot_general, dimension_numbers=NT, preferred_element_type=jnp.float32)
    return dot(a[0], b[0]) + (dot(a[0], b[1]) + dot(a[1], b[0]))


def blocks(count, mode, rank):
    quarter = rank // 4
    if mode == "d":
        return [(m * quarter, quarter, (), m) for m in range(count)]
    half = quarter // 2
    return [((r3 * count + m) * half, half, (r3,), m) for r3 in range(2) for m in range(count)]


def offset(me, bits, rel, block):
    total = 0
    size = block
    for bit, r in zip(bits, rel):
        size //= 2
        mine = bit_of(me, bit)
        total = total + (mine if r == 0 else 1 - mine) * size
    return total


def weighted(items, base, dirs_ref, res_ref, f2t, rows):
    parts = []
    for kind, probe in items:
        w = (dirs_ref if kind == 0 else res_ref)[pl.ds(base + probe, 1), rows]
        parts.append((f2t * w).astype(jnp.bfloat16))
    return jnp.concatenate(parts, axis=0)


def open_kernel(items, half, s_ref, f1_in, f2_in, dirs_in, res_in, out_ref, f1_ref, f2t_ref, dirs_ref, res_ref, f2_ref, sems):
    base = (1 - bit_of(s_ref[0], 0)) * half
    size = f1_in.shape[0] // LOADS
    small = [
        pltpu.make_async_copy(dirs_in, dirs_ref, sems.at[0]),
        pltpu.make_async_copy(res_in, res_ref, sems.at[1]),
    ]
    big = []
    for i in range(LOADS):
        part = pl.ds(i * size, size)
        big.append((
            pltpu.make_async_copy(f2_in.at[part], f2_ref.at[part], sems.at[2 + 2 * i]),
            pltpu.make_async_copy(f1_in.at[part], f1_ref.at[part], sems.at[3 + 2 * i]),
        ))
    for copy in small + [c for two in big for c in two]:
        copy.start()
    for copy in small:
        copy.wait()
    for k in range(f1_in.shape[0] // TILE):
        if k * TILE % size == 0:
            for copy in big[k * TILE // size]:
                copy.wait()
        rows = pl.ds(k * TILE, TILE)
        f2t = f2_ref[rows, :].astype(jnp.float32).T
        f2t_ref[:, rows] = f2t.astype(jnp.bfloat16)
        st = weighted(items, base, dirs_ref, res_ref, f2t, rows)
        r = jnp.dot(st, f1_ref[rows, :], preferred_element_type=jnp.float32)
        if k == 0:
            out_ref[...] = r
        else:
            out_ref[...] += r


def open_build(items, half, me, f1, f2, dirs, res):
    n, rank = f1.shape
    m = len(items)
    hbm = pl.BlockSpec(memory_space=pltpu.HBM)
    return pl.pallas_call(
        functools.partial(open_kernel, items, half),
        out_shape=[
            jax.ShapeDtypeStruct((m * rank, rank), jnp.float32),
            jax.ShapeDtypeStruct((n, rank), jnp.bfloat16),
            jax.ShapeDtypeStruct((rank, n), jnp.bfloat16),
            jax.ShapeDtypeStruct(dirs.shape, jnp.float32),
            jax.ShapeDtypeStruct(res.shape, jnp.float32),
        ],
        in_specs=[SMEM] + [hbm] * 4,
        out_specs=[VMEM] * 5,
        scratch_shapes=[pltpu.VMEM((n, rank), jnp.bfloat16), pltpu.SemaphoreType.DMA((2 + 2 * LOADS,))],
        compiler_params=pltpu.CompilerParams(vmem_limit_bytes=10 << 20),
        name="cores_open",
        cost_estimate=pl.CostEstimate(flops=2 * m * n * rank * rank, bytes_accessed=n * rank * 4, transcendentals=0),
    )(me, *(pltpu.with_memory_space_constraint(x, pltpu.HBM) for x in (f1, f2, dirs, res)))


def core_kernel(items, mine, half, s_ref, f1_ref, f2t_ref, dirs_ref, res_ref, *refs):
    out_ref = refs[-1]
    core = bit_of(s_ref[0], 0)
    base = (core if mine else 1 - core) * half
    for k in range(f1_ref.shape[0] // TILE):
        rows = pl.ds(k * TILE, TILE)
        st = weighted(items, base, dirs_ref, res_ref, f2t_ref[:, rows].astype(jnp.float32), rows)
        r = jnp.dot(st, f1_ref[rows, :], preferred_element_type=jnp.float32)
        if k == 0:
            out_ref[...] = r
        else:
            out_ref[...] += r


def build(items, mine, half, after, me, f1, f2t, dirs, res):
    n, rank = f1.shape
    m = len(items)
    extra = [] if after is None else [after]
    return pl.pallas_call(
        functools.partial(core_kernel, items, mine, half),
        out_shape=jax.ShapeDtypeStruct((m * rank, rank), jnp.float32),
        in_specs=[SMEM] + [VMEM] * 4 + [pl.BlockSpec(memory_space=pl.ANY)] * len(extra),
        out_specs=VMEM,
        compiler_params=pltpu.CompilerParams(vmem_limit_bytes=8 << 20),
        cost_estimate=pl.CostEstimate(flops=2 * m * n * rank * rank, bytes_accessed=n * rank * 4, transcendentals=0),
    )(me, f1, f2t, dirs, res, *extra)


def left_kernel(items, bits, mode, s_ref, a_ref, b_ref, m1_ref, q0, q1, q2, q3, scr):
    me = s_ref[0]
    qs = (q0, q1, q2, q3)
    rank = m1_ref.shape[0]
    m = len(items)
    m1 = m1_ref[...]
    sides = (split(m1), split(m1.T))
    for j, (kind, _) in enumerate(items):
        ct = a_ref[j * rank:(j + 1) * rank, :] + b_ref[j * rank:(j + 1) * rank, :]
        scr[j * rank:(j + 1) * rank, :] = dot3(sides[kind], split(ct))
    for r1 in range(2):
        for r2 in range(2):
            for row, size, r3, j in blocks(m, mode, rank):
                off = pl.multiple_of(offset(me, bits, (r1, r2) + r3, rank), 32)
                qs[r1 * 2 + r2][row:row + size, :] = scr[pl.ds(j * rank + off, size), :]


def left(items, bits, mode, me, own, got, m1):
    rank = m1.shape[0]
    m = len(items)
    return pl.pallas_call(
        functools.partial(left_kernel, items, bits, mode),
        out_shape=[jax.ShapeDtypeStruct((m * rank // 4, rank), jnp.float32)] * 4,
        in_specs=[SMEM] + [VMEM] * 3,
        out_specs=[VMEM] * 4,
        scratch_shapes=[pltpu.VMEM((m * rank, rank), jnp.float32)],
        compiler_params=pltpu.CompilerParams(vmem_limit_bytes=8 << 20),
        name="left",
        cost_estimate=pl.CostEstimate(flops=6 * m * rank**3, bytes_accessed=12 * m * rank * rank, transcendentals=0),
    )(me, own, got, m1)


def right_kernel(items, a_ref, b_ref, m2_ref, out_ref):
    rows = a_ref.shape[0] // len(items)
    m2 = m2_ref[...]
    sides = (split(m2), split(m2.T))
    for j, (kind, _) in enumerate(items):
        at = pl.ds(j * rows, rows)
        out_ref[at, :] = dot3(split(a_ref[at, :] + b_ref[at, :]), sides[kind])


def right(items, a, b, m2):
    return pl.pallas_call(
        functools.partial(right_kernel, items),
        out_shape=jax.ShapeDtypeStruct(a.shape, jnp.float32),
        in_specs=[VMEM] * 3,
        out_specs=VMEM,
        compiler_params=pltpu.CompilerParams(vmem_limit_bytes=4 << 20),
        name="right",
        cost_estimate=pl.CostEstimate(flops=6 * a.size * a.shape[1], bytes_accessed=12 * a.size, transcendentals=0),
    )(a, b, m2)


def apply_kernel(parts, half, first, last, *refs):
    s_ref, f1_ref, f2t_ref, dirs_ref, res_ref = refs[:5]
    pos = 5
    arrays = []
    for p in parts:
        arrays.append(refs[pos:pos + len(p[4])])
        pos += len(p[4])
    if not first:
        acc_in, prod_in = refs[pos:pos + 2]
        pos += 2
    acc_ref, prod_ref = refs[pos:pos + 2]
    pos += 2
    if last:
        acc_ref, grad_ref = acc_in, acc_ref
    if first:
        f1t_ref = refs[pos]
        pos += 1
        acc_ref[...] = jnp.zeros_like(acc_ref)
        prod_ref[...] = jnp.zeros_like(prod_ref)
    else:
        f1t_ref = f1_ref
        prod_ref[...] = prod_in[...]
    g_ref, r_ref = refs[pos:pos + 2]
    me = s_ref[0]
    core = bit_of(me, 0)
    rank = f2t_ref.shape[0]
    at = 0
    spans = []
    for four in arrays:
        for f in four:
            g_ref[at:at + f.shape[0], :] = f[...].astype(jnp.bfloat16)
            spans.append((at, f.shape[0]))
            at += f.shape[0]

    def tile(k):
        rows = pl.ds(k * TILE, TILE)
        r_ref[k % 2] = jnp.dot(g_ref[...], f2t_ref[:, rows], preferred_element_type=jnp.float32)
        if first:
            f1t_ref[:, rows] = f1_ref[rows, :].astype(jnp.float32).T
        span = iter(spans)
        for items, bits, mode, mine, quarters in parts:
            base = (core if mine else 1 - core) * half
            w = [(res_ref if kind == 0 else dirs_ref)[pl.ds(base + probe, 1), rows] for kind, probe in items]
            prods = [None] * len(items)
            for q in quarters:
                start, _ = next(span)
                sums = {}
                for row, size, r3, j in blocks(len(items), mode, rank):
                    block = r_ref[k % 2, start + row:start + row + size, :]
                    off = pl.multiple_of(offset(me, bits, (q // 2, q % 2) + r3, rank), 32)
                    term = block * w[j]
                    sums[r3] = (off, size, term if r3 not in sums else sums[r3][2] + term)
                    if items[j][0] == 0:
                        p = block * f1t_ref[pl.ds(off, size), rows]
                        p = jnp.sum(p.reshape(size // 8, 8, TILE), axis=0)
                        prods[j] = p if prods[j] is None else prods[j] + p
                for off, size, total in sums.values():
                    acc_ref[pl.ds(off, size), rows] += total
            for (kind, probe), p in zip(items, prods):
                if kind == 0:
                    prod_ref[pl.ds(base + probe, 1), rows] += jnp.sum(p, axis=0, keepdims=True)
        if last:
            grad_ref[rows, :] = acc_ref[:, rows].T

    for k in range(f2t_ref.shape[1] // TILE):
        tile(k)


def apply_cores(parts, half, me, f1, f2t, dirs, res, state, last):
    rank, n = f2t.shape
    first = state is None
    arrays = [a for p in parts for a in p[4].values()]
    shapes = [p[:4] + (tuple(p[4]),) for p in parts]
    total = sum(a.shape[0] for a in arrays)
    ops = [me, f1, f2t, dirs, res] + arrays + ([] if first else list(state))
    acc = jax.ShapeDtypeStruct((n, rank) if last else (rank, n), jnp.float32)
    outs = [acc, jax.ShapeDtypeStruct(dirs.shape, jnp.float32)]
    aliases = {}
    if first:
        outs.append(jax.ShapeDtypeStruct((rank, n), jnp.float32))
    elif not last:
        aliases = {len(ops) - 2: 0, len(ops) - 1: 1}
    return pl.pallas_call(
        functools.partial(apply_kernel, shapes, half, first, last),
        out_shape=outs,
        in_specs=[SMEM] + [VMEM] * (len(ops) - 1),
        out_specs=[VMEM] * len(outs),
        scratch_shapes=[pltpu.VMEM((total, rank), jnp.bfloat16), pltpu.VMEM((2, total, TILE), jnp.float32)],
        input_output_aliases=aliases,
        compiler_params=pltpu.CompilerParams(vmem_limit_bytes=16 << 20),
        name="apply_last" if last else "apply",
        cost_estimate=pl.CostEstimate(flops=2 * total * n * rank, bytes_accessed=8 * n * rank, transcendentals=0),
    )(*ops)


def shards(count, factor_one, factor_two, middle_one, middle_two, directions, residual):
    half = directions.shape[0] // 2
    extra = tuple(range(5, count.bit_length() - 1))

    def swap(x, *bits):
        mask = sum(1 << bit for bit in bits)
        return lax.ppermute(x, AXES, [(i, i ^ mask) for i in range(count)])

    me = (lax.axis_index("rows") * lax.axis_size("cores") + lax.axis_index("cores")).astype(jnp.int32).reshape(1)
    items = [(j % 2, j // 2) for j in range(2 * half)]
    groups = []
    at = 0
    for i, (size, bits, mode, back) in enumerate(GROUPS):
        size = len(items) - at if i == len(GROUPS) - 1 else size
        groups.append((tuple(items[at:at + size]), bits, mode, back))
        at += size

    other, f1, f2t, dirs, res = open_build(groups[0][0], half, me, factor_one, factor_two, directions, residual)
    args = (me, f1, f2t, dirs, res)
    others = [swap(other, 0)]
    q, after = [], None
    for g, (its, bits, mode, _) in enumerate(groups):
        own = build(its, True, half, after, *args)
        if g + 1 < len(groups):
            other = build(groups[g + 1][0], False, half, own, *args)
            others.append(swap(other, 0))
        q.append(left(its, bits, mode, me, own, others[g], middle_one))
        after = q[-1][3]
    t = [{} for _ in groups]
    for (_, bits, mode, _), v, x in zip(groups, t, q):
        v["r11"] = swap(x[3], bits[0])
    for (_, bits, mode, _), v, x in zip(groups, t, q):
        v["r10"] = swap(x[2], bits[0])
    for (_, bits, mode, _), v, x in zip(groups, t, q):
        v["r01"] = swap(x[1] + v["r11"], bits[1])
    for (_, bits, mode, _), v, x in zip(groups, t, q):
        a, b, c = x[0], v["r10"], v["r01"]
        if mode == "h":
            h = a.shape[0] // 2
            v["k"] = (a[:h] + b[:h]) + c[:h]
            v["s"] = (a[h:] + b[h:]) + c[h:]
        else:
            v["s"] = v["k"] = (a + b) + c
        v["r3"] = swap(v["s"], bits[2])
    for (_, bits, mode, back), v in zip(groups, t):
        v["k"] = v["k"] + v["r3"]
        v["r4"] = swap(v["k"], bits[3])
    for bit in extra:
        for v in t:
            v["k"] = v["k"] + v["r4"]
            v["r4"] = swap(v["k"], bit)
    for (its, bits, mode, _), v in zip(groups, t):
        v["k"] = right(its, v["k"], v["r4"], middle_two)
        if mode == "h":
            v["k"] = jnp.concatenate([v["k"], swap(v["k"], bits[2])])
    for (_, bits, mode, back), v in zip(groups, t):
        v["f"] = {0: v["k"]}
        v["f"][1] = swap(v["k"], bits[1])
        v["f"][2] = swap(v["k"], bits[0])
    for (_, bits, mode, back), v in zip(groups, t):
        if back == "p":
            v["f"][3] = swap(v["f"][1], bits[0])
        else:
            v["f"][3] = swap(v["k"], bits[0], bits[1])
        v["o"] = {}
        for i in range(4):
            v["o"][i] = swap(v["f"][i], 0)
    state = None
    for i, stage in enumerate(STAGES):
        parts = []
        for mine in BOTH:
            for g, ((its, bits, mode, _), v) in enumerate(zip(groups, t)):
                arrays = v["f" if mine else "o"]
                quarters = {j: arrays[j] for h, j, m in stage if (h, m) == (g, mine)}
                if quarters:
                    parts.append((its, bits, mode, mine, quarters))
        state = apply_cores(
            parts, half, me, f1, f2t, dirs, res, state, i == len(STAGES) - 1
        )
        if i == 0:
            f1, state = state[2], state[:2]
    gradient, products = state
    return products, gradient


def whole(count, *args):
    return shards(count, *args)


def solution(mesh):
    placed = (
        P(AXES, None),
        P(AXES, None),
        P(),
        P(),
        P(None, AXES),
        P(None, AXES),
    )
    count = mesh.shape["rows"] * mesh.shape["cores"]
    return jax.shard_map(
        functools.partial(whole, count),
        mesh=mesh,
        in_specs=placed,
        out_specs=(P(None, AXES), P(AXES, None)),
        check_vma=False,
    )
```
